32 devices in a mesh: seq: 8 (over z, x), head: 4 (over y, core).
Axes of the slice: x: 2, y: 2, z: 4, core: 2. Of those that a mesh axis runs over, the one named last changes fastest.
Arguments:
- block_input: bfloat16 [4096, 1024], P('seq'), may hold values from -6 to 6
- norm1_gain: float32 [1024], replicated, may hold values from 0.5 to 1.5
- w_in: bfloat16 [1024, 8, 768], P(None, 'head'), may hold values from -0.1875 to 0.1875
- w_ba: bfloat16 [1024, 2, 8], P(None, None, 'head'), may hold values from -0.1875 to 0.1875
- conv_weight: float32 [512, 8, 4], P(None, 'head'), may hold values from -2.5 to 2.5
- decay_log: float32 [8], P('head'), may hold values from -9 to -3.5
- gnorm_gain: float32 [256], replicated, may hold values from 0.5 to 1.5
- w_out: bfloat16 [256, 8, 1024], P(None, 'head'), may hold values from -0.1875 to 0.1875
- norm2_gain: float32 [1024], replicated, may hold values from 0.5 to 1.5
- w_up: bfloat16 [1024, 2, 2816], P(None, None, 'head'), may hold values from -0.1875 to 0.1875
- w_down: bfloat16 [1024, 2816], P(None, 'head'), may hold values from -0.15625 to 0.15625
- grad_out: bfloat16 [4096, 1024], P('seq'), may hold values from -6 to 6
Outputs:
- result: float32 [4096, 1024], P('seq')
- input_grad: float32 [4096, 1024], P('seq')
- norm1_gain_grad: float32 [1024], replicated
- input_weight_gradient: float32 [1024, 8, 768], P('seq', 'head')
- w_ba_grad: float32 [1024, 2, 8], P('seq', None, 'head')
- conv_grad: float32 [512, 8, 4], P('seq', 'head')
- log_decay_gradient: float32 [8], P('head')
- gnorm_gain_grad: float32 [256], replicated
- w_out_grad: float32 [256, 8, 1024], P('seq', 'head')
- norm2_gain_grad: float32 [1024], replicated
- w_up_grad: float32 [1024, 2, 2816], P('seq', None, 'head')
- w_down_grad: float32 [1024, 2816], P('seq', 'head')
The draws below stay inside these ranges and needn't reach their ends.
All inputs are finite; a program needn't handle non-finite values.
Results may differ from the reference program's by a relative error of at most 0.025.
The reference program's roundings to bfloat16 on the way (of `normed`, `projected`, `gated_out`, `hidden_n`, `swish`, `gate_up_grad`, `stream_b` and `proj_grad`) count: a program that leaves them out, or rounds other values in their place, can miss the bound.
Values may be sent and summed in bfloat16 or wider, within the bound.
A program may use at most 128 MiB of HBM per device.

```python
import jax
import jax.numpy as jnp
from jax import lax

D = 1024
H = 8
DK = 128
DV = 256
FF = 2816
CONV = 4
STRETCH = 64
TOKENS = 4096
N_HEAD = 4


def level_of(own_key, shape, cuts, low, largest):
    def one(position, blocks):
        draws = jax.random.uniform(jax.random.fold_in(jax.random.fold_in(own_key, 6), position), (blocks,), jnp.float32, low / len(cuts), largest / len(cuts))
        return jnp.repeat(jnp.exp(draws), shape[position] // blocks).reshape((-1,) + (1,) * (len(shape) - position - 1))

    factor_of = one(*cuts[0])
    for cut in cuts[1:]:
        factor_of = factor_of * one(*cut)
    return factor_of


def gaussian(stream_key, extent, scale, most, cuts=(), kind=jnp.bfloat16):
    drawn = scale * jax.random.normal(stream_key, extent, jnp.float32)
    if cuts:
        drawn = drawn * level_of(stream_key, extent, cuts, -0.22, 0.18)
    return jnp.clip(drawn, -most, most).astype(kind)


def setup_inputs(seed: int = 0) -> dict:
    seeds = jax.random.split(jax.random.key(seed), 13)
    block_input = gaussian(seeds[0], (TOKENS, D), 1.0, 6.0, ((0, 8),))
    norm1_gain = jnp.clip(1.0 + 0.1 * jax.random.normal(seeds[1], (D,), jnp.float32), 0.5, 1.5)
    w_in = gaussian(seeds[2], (D, H, 2 * DK + 2 * DV), D ** -0.5, 0.1875, ((1, 4),))
    w_ba = gaussian(seeds[3], (D, 2, H), D ** -0.5, 0.1875, ((2, 4),))
    conv_weight = gaussian(seeds[4], (2 * DK + DV, H, CONV), 0.5, 2.5, ((1, 4),), jnp.float32)
    decay_log = jnp.clip(-9.0 + 5.5 * jax.random.uniform(seeds[5], (H,), jnp.float32) ** level_of(seeds[5], (H,), ((0, 4),), -0.2, 0.2), -9.0, -3.5)
    gnorm_gain = jnp.clip(1.0 + 0.1 * jax.random.normal(seeds[6], (DV,), jnp.float32), 0.5, 1.5)
    w_out = gaussian(seeds[7], (DV, H, D), (H * DV // 2) ** -0.5, 0.1875, ((1, 4),))
    norm2_gain = jnp.clip(1.0 + 0.1 * jax.random.normal(seeds[8], (D,), jnp.float32), 0.5, 1.5)
    w_up = gaussian(seeds[9], (D, 2, FF), D ** -0.5, 0.1875, ((2, 4),))
    w_down = gaussian(seeds[10], (D, FF), (FF // 2) ** -0.5, 0.15625, ((1, 4),))
    grad_out = gaussian(seeds[11], (TOKENS, D), 1.0, 6.0, ((0, 8),))
    return {"block_input": block_input, "norm1_gain": norm1_gain, "w_in": w_in, "w_ba": w_ba, "conv_weight": conv_weight, "decay_log": decay_log, "gnorm_gain": gnorm_gain, "w_out": w_out, "norm2_gain": norm2_gain, "w_up": w_up, "w_down": w_down, "grad_out": grad_out}


EPSILON = 1e-06
NEGATIVE = -1e+30
MATMUL_ACCURACY = lax.Precision.HIGHEST

def dot_high(left, right):
    return jnp.dot(left, right, precision=MATMUL_ACCURACY)

def rms_apply(values, gain):
    return values * lax.rsqrt(lax.optimization_barrier(jnp.mean(values * values, axis=-1, keepdims=True)) + EPSILON) * gain

def features(edged, mixer_in, conv_weight, decay_log):
    length = edged.shape[0] - (CONV - 1)
    mixed = edged[0:length] * conv_weight[:, :, 0].T
    for index in range(1, CONV):
        mixed = mixed + edged[index:index + length] * conv_weight[:, :, index].T
    active = jax.nn.silu(mixed)
    query = active[..., :DK]
    key = active[..., DK:2 * DK]
    value = active[..., 2 * DK:]
    query = query * lax.rsqrt(lax.optimization_barrier(jnp.sum(query * query, axis=-1, keepdims=True)) + EPSILON) * DK ** (-0.5)
    key = key * lax.rsqrt(lax.optimization_barrier(jnp.sum(key * key, axis=-1, keepdims=True)) + EPSILON)
    beta = jax.nn.sigmoid(mixer_in[:, 0])
    logdecay = -jnp.exp(decay_log) * jax.nn.softplus(mixer_in[:, 1])
    return (query, key, value, beta, logdecay)

def stretch_terms(query, key, value, beta, logdecay):
    width = query.shape[0]
    cumul = jnp.cumsum(logdecay)
    spread = cumul[:, None] - cumul[None, :]
    row_pos = lax.broadcasted_iota(jnp.int32, (width, width), 0)
    column = lax.broadcasted_iota(jnp.int32, (width, width), 1)
    strict = jnp.exp(jnp.where(row_pos > column, spread, NEGATIVE))
    inclusive = jnp.exp(jnp.where(row_pos >= column, spread, NEGATIVE))
    lower = beta[:, None] * strict * dot_high(key, key.T)
    system = jnp.eye(width, dtype=query.dtype) + lower
    solved_value = jax.scipy.linalg.solve_triangular(system, beta[:, None] * value, lower=True, unit_diagonal=True)
    solved_key = jax.scipy.linalg.solve_triangular(system, (beta * jnp.exp(cumul))[:, None] * key, lower=True, unit_diagonal=True)
    scores = inclusive * dot_high(query, key.T)
    query_map = jnp.exp(cumul)[:, None] * query - dot_high(scores, solved_key)
    out_fixed = dot_high(scores, solved_value)
    key_end = jnp.exp(cumul[-1] - cumul)[:, None] * key
    transit = jnp.exp(cumul[-1]) * jnp.eye(key.shape[1], dtype=query.dtype) - dot_high(key_end.T, solved_key)
    feed = dot_high(key_end.T, solved_value)
    return (query_map, out_fixed, transit, feed)

def stretch_head(query, key, value, beta, logdecay):
    count = query.shape[0] // STRETCH

    def split(array):
        return array.reshape((count, STRETCH) + array.shape[1:])
    return jax.vmap(stretch_terms)(split(query), split(key), split(value), split(beta), split(logdecay))

def stretch_heads(query, key, value, beta, logdecay):
    return jax.vmap(stretch_head, in_axes=1, out_axes=0)(query, key, value, beta, logdecay)

def scan_head(terms, state):

    def advance(carry, parts):
        query_map, out_fixed, transit, feed = parts
        return (dot_high(transit, carry) + feed, dot_high(query_map, carry) + out_fixed)
    final, layer_outputs = lax.scan(advance, state, terms)
    return (layer_outputs.reshape(-1, state.shape[1]), final)

def scan_heads(terms, state):
    return jax.vmap(scan_head, in_axes=(0, 0), out_axes=(1, 0))(terms, state)

def gated(layer_outputs, gate, gain):
    return rms_apply(layer_outputs, gain) * jax.nn.silu(gate)

def swiglu(gate_up):
    return jax.nn.silu(gate_up[:, 0]) * gate_up[:, 1]

def group_total(left, right):
    part_width = left.shape[1] // N_HEAD
    total = jnp.zeros((left.shape[0], right.shape[1]), jnp.float32)
    for group in range(N_HEAD):
        part = jnp.dot(left[:, group * part_width:(group + 1) * part_width].astype(jnp.float32), right[group * part_width:(group + 1) * part_width].astype(jnp.float32), preferred_element_type=jnp.float32)
        rounded = lax.optimization_barrier(part.astype(jnp.bfloat16))
        total = total + rounded.astype(jnp.float32)
    return total

def reference(block_input, norm1_gain, w_in, w_ba, conv_weight, decay_log, gnorm_gain, w_out, norm2_gain, w_up, w_down, grad_out):
    length = block_input.shape[0]
    model = block_input.shape[1]
    heads = w_in.shape[1]
    span = w_in.shape[2]
    channels = conv_weight.shape[0]
    units = w_up.shape[2]
    tokens_wide = block_input.astype(jnp.float32)
    normed, pull_first = jax.vjp(rms_apply, tokens_wide, norm1_gain)
    normed_b = normed.astype(jnp.bfloat16)
    w_in_flat = w_in.reshape(model, heads * span)
    w_ba_flat = w_ba.reshape(model, 2 * heads)
    projected = jnp.dot(normed_b.astype(jnp.float32), w_in_flat.astype(jnp.float32), preferred_element_type=jnp.float32).astype(jnp.bfloat16).reshape(length, heads, span)
    mixer_in = jnp.dot(normed_b.astype(jnp.float32), w_ba_flat.astype(jnp.float32), preferred_element_type=jnp.float32).reshape(length, 2, heads)
    edged = jnp.concatenate([jnp.zeros((CONV - 1, heads, channels), jnp.float32), projected[:, :, :channels].astype(jnp.float32)], 0)
    feats, pull_feat = jax.vjp(features, edged, mixer_in, conv_weight, decay_log)
    terms, pull_terms = jax.vjp(stretch_heads, *feats)
    start = jnp.zeros((heads, DK, DV), jnp.float32)
    (layer_outputs, final), pull_scan = jax.vjp(scan_heads, terms, start)
    gate_wide = projected[:, :, channels:].astype(jnp.float32)
    gated_out, pull_gate = jax.vjp(gated, layer_outputs, gate_wide, gnorm_gain)
    gated_b = gated_out.astype(jnp.bfloat16).reshape(length, heads * DV)
    w_out_flat = w_out.transpose(1, 0, 2).reshape(heads * DV, model)
    mixed = group_total(gated_b, w_out_flat)
    hidden = tokens_wide + mixed
    hidden_n, pull_second = jax.vjp(rms_apply, hidden, norm2_gain)
    hidden_b = hidden_n.astype(jnp.bfloat16)
    w_up_flat = w_up.reshape(model, 2 * units)
    gate_up = jnp.dot(hidden_b.astype(jnp.float32), w_up_flat.astype(jnp.float32), preferred_element_type=jnp.float32).reshape(length, 2, units)
    swish, pull_swish = jax.vjp(swiglu, gate_up)
    swish_b = swish.astype(jnp.bfloat16)
    ffn_total = group_total(swish_b, w_down.T)
    result = hidden + ffn_total
    act_grad = jnp.dot(grad_out.astype(jnp.float32), w_down.astype(jnp.float32), preferred_element_type=jnp.float32)
    w_down_grad = jnp.dot(grad_out.T.astype(jnp.float32), swish_b.astype(jnp.float32), preferred_element_type=jnp.float32)
    gate_up_grad, = pull_swish(act_grad)
    gate_up_b = gate_up_grad.astype(jnp.bfloat16).reshape(length, 2 * units)
    w_up_grad = jnp.dot(hidden_b.T.astype(jnp.float32), gate_up_b.astype(jnp.float32), preferred_element_type=jnp.float32).reshape(model, 2, units)
    second_total = jnp.dot(gate_up_b.astype(jnp.float32), w_up_flat.T.astype(jnp.float32), preferred_element_type=jnp.float32)
    hidden_grad, norm2_gain_grad = pull_second(second_total)
    stream = grad_out.astype(jnp.float32) + hidden_grad
    stream_b = stream.astype(jnp.bfloat16)
    w_out_grad = jnp.dot(gated_b.T.astype(jnp.float32), stream_b.astype(jnp.float32), preferred_element_type=jnp.float32).reshape(heads, DV, model).transpose(1, 0, 2)
    gated_grad = jnp.dot(stream_b.astype(jnp.float32), w_out_flat.T.astype(jnp.float32), preferred_element_type=jnp.float32).reshape(length, heads, DV)
    output_gradient, gate_grad, gnorm_gain_grad = pull_gate(gated_grad)
    term_grad, start_grad = pull_scan((output_gradient, jnp.zeros_like(final)))
    feat_grad = pull_terms(term_grad)
    edged_grad, mixer_grad, conv_grad, log_decay_gradient = pull_feat(tuple(feat_grad))
    proj_grad = jnp.concatenate([edged_grad[CONV - 1:], gate_grad], 2).astype(jnp.bfloat16).reshape(length, heads * span)
    mixer_b = mixer_grad.astype(jnp.bfloat16).reshape(length, 2 * heads)
    input_weight_gradient = jnp.dot(normed_b.T.astype(jnp.float32), proj_grad.astype(jnp.float32), preferred_element_type=jnp.float32).reshape(model, heads, span)
    w_ba_grad = jnp.dot(normed_b.T.astype(jnp.float32), mixer_b.astype(jnp.float32), preferred_element_type=jnp.float32).reshape(model, 2, heads)
    first_total = jnp.dot(proj_grad.astype(jnp.float32), w_in_flat.T.astype(jnp.float32), preferred_element_type=jnp.float32) + jnp.dot(mixer_b.astype(jnp.float32), w_ba_flat.T.astype(jnp.float32), preferred_element_type=jnp.float32)
    input_part, norm1_gain_grad = pull_first(first_total)
    input_grad = stream + input_part
    return (result, input_grad, norm1_gain_grad, input_weight_gradient, w_ba_grad, conv_grad, log_decay_gradient, gnorm_gain_grad, w_out_grad, norm2_gain_grad, w_up_grad, w_down_grad)
```

```python
import jax
import jax.numpy as jnp
from jax import lax
from jax.sharding import PartitionSpec as P

DK = 128
DV = 256
CONV = 4
STRETCH = 64


EPSILON = 1e-06
NEGATIVE = -1e30
FINE = lax.Precision.HIGH


def shifted(block, axis, distance):
    devices = range(lax.axis_size(axis))
    route = [(i - distance, i) for i in devices if i - distance in devices]
    return lax.ppermute(block, axis, route)


def head_sum(part):
    return lax.psum(part.astype(jnp.bfloat16), "head")


def seq_share(grad):
    return lax.psum_scatter(
        grad.astype(jnp.bfloat16), "seq", scatter_dimension=0, tiled=True
    ).astype(jnp.float32)


def carried_states(part, reverse):
    count = lax.axis_size("seq")
    place = lax.axis_index("seq")
    gathered = lax.all_gather(part.astype(jnp.bfloat16), "seq")
    order = range(count - 1, 0, -1) if reverse else range(count - 1)
    state = jnp.zeros(part.shape[:-1] + (DV,), jnp.float32)
    for index, source in enumerate(order):
        feed = gathered[source, ..., DK:].astype(jnp.float32)
        if index:
            moved = (
                jnp.matmul(
                    gathered[source, ..., :DK],
                    state.astype(jnp.bfloat16),
                    preferred_element_type=jnp.float32,
                )
                + feed
            )
        else:
            moved = feed
        ahead = source > place if reverse else source < place
        state = jnp.where(ahead, moved, state)
    return state


def rms_apply(values, gain):
    return values * lax.rsqrt(jnp.mean(values * values, axis=-1, keepdims=True) + EPSILON) * gain


def features(edged, mixer_in, conv_weight, decay_log):
    length = edged.shape[1] - (CONV - 1)
    taps = jnp.transpose(conv_weight, (2, 1, 0))[:, :, None, :]
    mixed = edged[:, 0:length] * taps[0]
    for index in range(1, CONV):
        mixed = mixed + edged[:, index : index + length] * taps[index]
    active = jax.nn.silu(mixed)
    query = active[..., :DK]
    key = active[..., DK : 2 * DK]
    value = active[..., 2 * DK :]
    query = (
        query * lax.rsqrt(jnp.sum(query * query, axis=-1, keepdims=True) + EPSILON) * DK ** (-0.5)
    )
    key = key * lax.rsqrt(jnp.sum(key * key, axis=-1, keepdims=True) + EPSILON)
    beta = jax.nn.sigmoid(mixer_in[0])
    logdecay = -jnp.exp(decay_log)[:, None] * jax.nn.softplus(mixer_in[1])
    return (query, key, value, beta, logdecay)


def fine(left, right):
    return jnp.matmul(left, right, precision=FINE)


def flip(array):
    return jnp.swapaxes(array, -1, -2)


@jax.custom_vjp
def unit_inverse(lower):
    width = lower.shape[-1]
    row_pos = lax.broadcasted_iota(jnp.int32, (width, width), 0)
    column = lax.broadcasted_iota(jnp.int32, (width, width), 1)

    def pairs(size):
        return (row_pos // size == column // size + 1) & ((row_pos // size) % 2 == 1)

    inverse = jnp.eye(width, dtype=lower.dtype) - jnp.where(pairs(1), lower, 0.0)
    size = 2
    while size < width:
        inverse = inverse - fine(fine(inverse, jnp.where(pairs(size), lower, 0.0)), inverse)
        size *= 2
    return inverse


def unit_inverse_fwd(lower):
    inverse = unit_inverse(lower)
    return inverse, inverse


def unit_inverse_bwd(inverse, grad):
    turned = flip(inverse)
    return (-fine(fine(turned, grad), turned),)


unit_inverse.defvjp(unit_inverse_fwd, unit_inverse_bwd)


def stretch_terms(query, key, value, beta, logdecay):
    width = query.shape[-2]
    row_pos = lax.broadcasted_iota(jnp.int32, (width, width), 0)
    column = lax.broadcasted_iota(jnp.int32, (width, width), 1)
    upto = (row_pos >= column).astype(jnp.float32)
    cumul = jnp.sum(upto * logdecay[..., None, :], axis=-1)
    last = jnp.sum(logdecay, axis=-1)[..., None, None]
    spread = cumul[..., :, None] - cumul[..., None, :]
    decay = jnp.exp(jnp.where(row_pos >= column, spread, NEGATIVE))
    strict = jnp.where(row_pos > column, decay, 0.0)
    lower = beta[..., None] * strict * fine(key, flip(key))
    inverse = unit_inverse(lower)
    growth = jnp.exp(cumul)[..., None]
    sides = jnp.concatenate(
        [(beta[..., None] * growth) * key, beta[..., None] * value], axis=-1
    )
    solved = jnp.matmul(inverse, sides)
    scores = decay * jnp.matmul(query, flip(key))
    mapped = jnp.matmul(scores, solved)
    query_map = growth * query - mapped[..., :DK]
    out_fixed = mapped[..., DK:]
    key_end = jnp.exp(last - cumul[..., None]) * key
    ended = jnp.matmul(flip(key_end), solved)
    transit = jnp.exp(last) * jnp.eye(DK, dtype=query.dtype) - ended[..., :DK]
    feed = ended[..., DK:]
    return (query_map, out_fixed, transit, feed)


def gated(layer_outputs, gate, gain):
    return rms_apply(layer_outputs, gain) * jax.nn.silu(gate)


def swiglu(gate_up):
    return jax.nn.silu(gate_up[:, 0]) * gate_up[:, 1]


def chain(maps, feeds):
    start = jnp.concatenate(
        [
            jnp.broadcast_to(jnp.eye(DK, dtype=jnp.float32), maps[0].shape),
            jnp.zeros_like(feeds[0]),
        ],
        axis=-1,
    )
    pad = ((0, 0), (0, 0), (DK, 0))
    states = [start]
    for index, (part, feed) in enumerate(zip(maps, feeds)):
        if index == 0:
            states.append(jnp.concatenate([part, feed], axis=-1))
        else:
            states.append(fine(part, states[-1]) + jnp.pad(feed, pad))
    return states


def shards(
    block_input,
    norm1_gain,
    w_in,
    w_ba,
    conv_weight,
    decay_log,
    gnorm_gain,
    w_out,
    norm2_gain,
    w_up,
    w_down,
    grad_out,
):
    length = block_input.shape[0]
    heads = w_in.shape[1]
    channels = conv_weight.shape[0]
    blocks = length // STRETCH
    f32 = jnp.float32
    bf16 = jnp.bfloat16

    def split(array):
        return array.reshape((heads, blocks, STRETCH) + array.shape[2:])

    tokens_wide = block_input.astype(f32)
    normed, pull_first = jax.vjp(rms_apply, tokens_wide, norm1_gain)
    normed_b = normed.astype(bf16)
    projected = jnp.einsum(
        "td,dhc->htc", normed_b, w_in, preferred_element_type=f32
    ).astype(bf16)
    mixer_in = jnp.einsum("td,dch->cht", normed_b, w_ba, preferred_element_type=f32)
    edge = shifted(projected[:, length - (CONV - 1) :, :channels], "seq", 1)
    edged = jnp.concatenate([edge, projected[:, :, :channels]], 1).astype(f32)
    feats, pull_feat = jax.vjp(features, edged, mixer_in, conv_weight, decay_log)
    terms, pull_terms = jax.vjp(stretch_terms, *[split(a) for a in feats])
    query_map, out_fixed, transit, feed = terms
    starts = chain(
        [transit[:, i] for i in range(blocks)], [feed[:, i] for i in range(blocks)]
    )
    carried = carried_states(starts[-1], False)
    before = jnp.stack(starts[:-1], axis=1)
    states = jnp.matmul(before[..., :DK], carried[:, None]) + before[..., DK:]
    layer_outputs = (jnp.matmul(query_map, states) + out_fixed).reshape(heads, length, DV)
    gate_wide = projected[:, :, channels:].astype(f32)
    gated_out, pull_gate = jax.vjp(gated, layer_outputs, gate_wide, gnorm_gain)
    gated_b = gated_out.astype(bf16)
    mixer_part = jnp.einsum("htc,chd->td", gated_b, w_out, preferred_element_type=f32)
    mixed = head_sum(mixer_part).astype(f32)
    hidden = tokens_wide + mixed
    hidden_n, pull_second = jax.vjp(rms_apply, hidden, norm2_gain)
    hidden_b = hidden_n.astype(bf16)
    gate_up = jnp.einsum("td,dcf->tcf", hidden_b, w_up, preferred_element_type=f32)
    swish, pull_swish = jax.vjp(swiglu, gate_up)
    swish_b = swish.astype(bf16)
    act_grad = jnp.dot(grad_out, w_down, preferred_element_type=f32)
    (gate_up_grad,) = pull_swish(act_grad)
    gate_up_b = gate_up_grad.astype(bf16)
    second_part = jnp.einsum("tcf,dcf->td", gate_up_b, w_up, preferred_element_type=f32)
    second_total = head_sum(second_part).astype(f32)
    down_grad = lax.dot_general(
        grad_out, swish_b, (((0,), (0,)), ((), ())), preferred_element_type=f32
    )
    up_grad = jnp.einsum("td,tcf->dcf", hidden_b, gate_up_b, preferred_element_type=f32)
    up_share = seq_share(up_grad)
    down_share = seq_share(down_grad)
    hidden_grad, gain_second = pull_second(second_total)
    stream = grad_out.astype(f32) + hidden_grad
    stream_b = stream.astype(bf16)
    gated_grad = jnp.einsum("td,chd->htc", stream_b, w_out, preferred_element_type=f32)
    output_gradient, gate_grad, gain_gated = pull_gate(gated_grad)
    out_weight_grad = jnp.einsum("htc,td->chd", gated_b, stream_b, preferred_element_type=f32)
    out_share = seq_share(out_weight_grad)
    out_split = split(output_gradient)
    back_feed = jnp.matmul(flip(query_map), out_split)
    turned = flip(transit)
    backs = chain(
        [turned[:, i] for i in reversed(range(blocks))],
        [back_feed[:, i] for i in reversed(range(blocks))],
    )
    later_grad = carried_states(backs[-1], True)
    after = jnp.stack(backs[:-1][::-1], axis=1)
    later = jnp.matmul(after[..., :DK], later_grad[:, None]) + after[..., DK:]
    term_grad = (
        jnp.matmul(out_split, flip(states)),
        out_split,
        jnp.matmul(later, flip(states)),
        later,
    )
    feat_grad = [
        a.reshape((heads, length) + a.shape[3:]) for a in pull_terms(term_grad)
    ]
    edged_grad, mixer_grad, conv_grad, log_decay_gradient = pull_feat(tuple(feat_grad))
    back_edge = shifted(edged_grad[:, : CONV - 1], "seq", -1)
    channel_grad = edged_grad[:, CONV - 1 :]
    channel_grad = jnp.concatenate(
        [
            channel_grad[:, : length - (CONV - 1)],
            channel_grad[:, length - (CONV - 1) :] + back_edge,
        ],
        1,
    )
    proj_grad = jnp.concatenate([channel_grad, gate_grad], 2).astype(bf16)
    mixer_b = mixer_grad.astype(bf16)
    first_part = jnp.einsum("htc,dhc->td", proj_grad, w_in, preferred_element_type=f32)
    first_part = first_part + jnp.einsum(
        "cht,dch->td", mixer_b, w_ba, preferred_element_type=f32
    )
    first_total = head_sum(first_part).astype(f32)
    ffn_part = lax.dot_general(
        swish_b, w_down, (((1,), (1,)), ((), ())), preferred_element_type=f32
    )
    result = hidden + head_sum(ffn_part).astype(f32)
    in_weight_grad = jnp.einsum("td,htc->dhc", normed_b, proj_grad, preferred_element_type=f32)
    in_share = seq_share(in_weight_grad)
    gate_weight_grad = jnp.einsum("td,cht->dch", normed_b, mixer_b, preferred_element_type=f32)
    input_part, gain_first = pull_first(first_total)
    input_grad = stream + input_part
    small = [
        gain_first,
        gain_second,
        lax.psum(gain_gated, "head"),
        log_decay_gradient,
        conv_grad.reshape(-1),
        gate_weight_grad.reshape(-1),
    ]
    summed = lax.psum(jnp.concatenate(small), "seq")
    pieces, at = [], 0
    for part in small:
        pieces.append(summed[at : at + part.shape[0]])
        at += part.shape[0]
    gain_one, gain_two, gain_norm, decay_total, conv_total, gate_total = pieces
    count = lax.axis_size("seq")
    place = lax.axis_index("seq")

    def mine(flat, shape):
        share = flat.shape[0] // count
        piece = lax.dynamic_slice(flat, (place * share,), (share,))
        return piece.reshape((shape[0] // count,) + shape[1:])

    return (
        result,
        input_grad,
        gain_one,
        in_share,
        mine(gate_total, gate_weight_grad.shape),
        mine(conv_total, conv_grad.shape),
        decay_total,
        gain_norm,
        out_share,
        gain_two,
        up_share,
        down_share,
    )


def solution(mesh):
    return jax.shard_map(
        shards,
        mesh=mesh,
        in_specs=(
            P("seq", None),
            P(),
            P(None, "head", None),
            P(None, None, "head"),
            P(None, "head", None),
            P("head"),
            P(),
            P(None, "head", None),
            P(),
            P(None, None, "head"),
            P(None, "head"),
            P("seq", None),
        ),
        out_specs=(
            P("seq", None),
            P("seq", None),
            P(),
            P("seq", "head", None),
            P("seq", None, "head"),
            P("seq", "head", None),
            P("head"),
            P(),
            P("seq", "head", None),
            P(),
            P("seq", None, "head"),
            P("seq", "head"),
        ),
        check_vma=False,
    )
```

```python
import functools

import jax
import jax.numpy as jnp
from jax import lax
from jax.experimental import pallas as pl
from jax.experimental.pallas import tpu as pltpu
from jax.sharding import PartitionSpec as P

DK = 128
DV = 256
CONV = 4
STRETCH = 64


EPSILON = 1e-06
NEGATIVE = -1e30
FINE = lax.Precision.HIGH


def shifted(block, axis, distance):
    devices = range(lax.axis_size(axis))
    route = [(i - distance, i) for i in devices if i - distance in devices]
    return lax.ppermute(block, axis, route)


MESH = pl.DeviceIdType.MESH
PIECES = 4


def flipped(index, bit):
    mine = (index // bit) % 2
    return index + bit - 2 * bit * mine, mine


def powers(count):
    return [2**i for i in range(count.bit_length() - 1)]


def greet(axis, partners):
    barrier = pltpu.get_barrier_semaphore()
    for partner in partners:
        pl.semaphore_signal(barrier, inc=1, device_id={axis: partner}, device_id_type=MESH)
    pl.semaphore_wait(barrier, len(partners))


def head_sum_kernel(
    count, x_ref, out_ref, first, held, sums, near_s, near_r, far_s, far_r, back_s, back_r
):
    me = lax.axis_index("head")
    bits = powers(count)
    partner, side = flipped(me, 1)
    peers = [flipped(me, bit)[0] for bit in bits[1:]]
    greet("head", [partner] + peers)

    def send(src, dst, send_sem, recv_sem, device):
        copy = pltpu.make_async_remote_copy(
            src_ref=src,
            dst_ref=dst,
            send_sem=send_sem,
            recv_sem=recv_sem,
            device_id={"head": device},
            device_id_type=MESH,
        )
        copy.start()
        return copy

    def add(left, right):
        return (left.astype(jnp.float32) + right.astype(jnp.float32)).astype(jnp.bfloat16)

    near = [
        send(x_ref.at[1 - side, k], first.at[k], near_s.at[k], near_r.at[k], partner)
        for k in range(PIECES)
    ]
    steps = len(peers)
    copies = []
    for k in range(PIECES):
        near[k].wait()
        sums[0, k] = add(x_ref[side, k], first[k])
        copies.append(
            send(sums.at[0, k], held.at[0, k], far_s.at[0, k], far_r.at[0, k], peers[0])
        )
    for step in range(steps):
        later = []
        for k in range(PIECES):
            copies[k].wait()
            total = add(sums[step, k], held[step, k])
            if step < steps - 1:
                sums[step + 1, k] = total
                later.append(
                    send(
                        sums.at[step + 1, k],
                        held.at[step + 1, k],
                        far_s.at[step + 1, k],
                        far_r.at[step + 1, k],
                        peers[step + 1],
                    )
                )
            else:
                out_ref[side, k] = total
                later.append(
                    send(
                        out_ref.at[side, k],
                        out_ref.at[side, k],
                        back_s.at[k],
                        back_r.at[k],
                        partner,
                    )
                )
        copies = later
    for copy in copies:
        copy.wait()


def head_sum(part):
    count = lax.axis_size("head")
    rows, width = part.shape
    steps = len(powers(count)) - 1
    piece = (rows // (2 * PIECES), width)
    whole = (2, PIECES) + piece
    dma = pltpu.SemaphoreType.DMA
    total = pl.pallas_call(
        functools.partial(head_sum_kernel, count),
        out_shape=jax.ShapeDtypeStruct(whole, jnp.bfloat16),
        in_specs=[pl.BlockSpec(memory_space=pltpu.VMEM)],
        out_specs=pl.BlockSpec(memory_space=pltpu.VMEM),
        scratch_shapes=[
            pltpu.VMEM((PIECES,) + piece, jnp.bfloat16),
            pltpu.VMEM((steps, PIECES) + piece, jnp.bfloat16),
            pltpu.VMEM((steps, PIECES) + piece, jnp.bfloat16),
            dma((PIECES,)),
            dma((PIECES,)),
            dma((steps, PIECES)),
            dma((steps, PIECES)),
            dma((PIECES,)),
            dma((PIECES,)),
        ],
        compiler_params=pltpu.CompilerParams(
            collective_id=0, has_side_effects=True, vmem_limit_bytes=16 << 20
        ),
        name="head_sum",
    )(part.astype(jnp.bfloat16).reshape(whole))
    return total.reshape(rows, width)


def seq_share_kernel(count, arrays, *refs):
    x_refs, out_refs = refs[:arrays], refs[arrays : 2 * arrays]
    scratch = refs[2 * arrays :]
    recv_refs, send_refs = scratch[:arrays], scratch[arrays : 2 * arrays]
    send_sem, recv_sem = scratch[2 * arrays :]
    me = lax.axis_index("seq")
    bits = powers(count)
    partners = {bit: flipped(me, bit)[0] for bit in bits}
    greet("seq", [partners[bit] for bit in bits])

    def block(relative):
        index = me
        for bit in bits:
            if relative & bit:
                index = flipped(index, bit)[0]
        return index

    orders = [bits, bits[1:] + bits[:1]]
    works = []
    for a in range(arrays):
        half = x_refs[a].shape[1] // 2
        for way in range(2):
            works.append((a, way, pl.ds(way * half, half)))

    def kept(order, step):
        used = sum(order[:step])
        return [r for r in range(count) if r & used == 0]

    def partial_sum(work, relative, step):
        a, way, rows = work
        total = x_refs[a][block(relative), rows, :].astype(jnp.float32)
        for earlier in range(step):
            total = total + recv_refs[a][way, earlier, slot(way, earlier, relative)].astype(
                jnp.float32
            )
        return total

    def slot(way, step, relative):
        return kept(orders[way], step + 1).index(relative)

    pending = {}
    for step in range(len(bits) + 1):
        for number, work in enumerate(works):
            a, way, rows = work
            order = orders[way]
            for copy in pending.pop(number, []):
                copy.wait()
            if step == len(bits):
                out_refs[a][rows, :] = partial_sum(work, 0, step)
                continue
            bit = order[step]
            started = []
            for relative in kept(order, step):
                if not relative & bit:
                    continue
                place = slot(way, step, relative - bit)
                if step == 0:
                    source = x_refs[a].at[block(relative), rows, :]
                else:
                    send_refs[a][way, step - 1, place] = partial_sum(
                        work, relative, step
                    ).astype(jnp.bfloat16)
                    source = send_refs[a].at[way, step - 1, place]
                copy = pltpu.make_async_remote_copy(
                    src_ref=source,
                    dst_ref=recv_refs[a].at[way, step, place],
                    send_sem=send_sem.at[number, step, place],
                    recv_sem=recv_sem.at[number, step, place],
                    device_id={"seq": partners[bit]},
                    device_id_type=MESH,
                )
                copy.start()
                started.append(copy)
            pending[number] = started


def seq_shares(grads):
    count = lax.axis_size("seq")
    steps = len(powers(count))
    blocks = [
        g.astype(jnp.bfloat16).reshape(count, g.shape[0] // count, g.shape[1]) for g in grads
    ]
    halves = [(b.shape[1] // 2, b.shape[2]) for b in blocks]
    works = 2 * len(grads)
    vmem = pl.BlockSpec(memory_space=pltpu.VMEM)
    return pl.pallas_call(
        functools.partial(seq_share_kernel, count, len(grads)),
        out_shape=[jax.ShapeDtypeStruct(b.shape[1:], jnp.float32) for b in blocks],
        in_specs=[vmem] * len(grads),
        out_specs=[vmem] * len(grads),
        scratch_shapes=[
            pltpu.VMEM((2, steps, count // 2) + half, jnp.bfloat16) for half in halves
        ]
        + [pltpu.VMEM((2, max(steps - 1, 1), count // 4) + half, jnp.bfloat16) for half in halves]
        + [
            pltpu.SemaphoreType.DMA((works, steps, count // 2)),
            pltpu.SemaphoreType.DMA((works, steps, count // 2)),
        ],
        compiler_params=pltpu.CompilerParams(
            collective_id=1, has_side_effects=True, vmem_limit_bytes=48 << 20
        ),
        name="seq_shares",
    )(*blocks)


def seq_share(grad):
    return lax.psum_scatter(
        grad.astype(jnp.bfloat16), "seq", scatter_dimension=0, tiled=True
    ).astype(jnp.float32)


def carried_states(part, reverse):
    count = lax.axis_size("seq")
    place = lax.axis_index("seq")
    gathered = lax.all_gather(part.astype(jnp.bfloat16), "seq")
    order = range(count - 1, 0, -1) if reverse else range(count - 1)
    state = jnp.zeros(part.shape[:-1] + (DV,), jnp.float32)
    for index, source in enumerate(order):
        feed = gathered[source, ..., DK:].astype(jnp.float32)
        if index:
            moved = (
                jnp.matmul(
                    gathered[source, ..., :DK],
                    state.astype(jnp.bfloat16),
                    preferred_element_type=jnp.float32,
                )
                + feed
            )
        else:
            moved = feed
        ahead = source > place if reverse else source < place
        state = jnp.where(ahead, moved, state)
    return state


def rms_apply(values, gain):
    return values * lax.rsqrt(jnp.mean(values * values, axis=-1, keepdims=True) + EPSILON) * gain


def features(edged, mixer_in, conv_weight, decay_log):
    length = edged.shape[1] - (CONV - 1)
    taps = jnp.transpose(conv_weight, (2, 1, 0))[:, :, None, :]
    mixed = edged[:, 0:length] * taps[0]
    for index in range(1, CONV):
        mixed = mixed + edged[:, index : index + length] * taps[index]
    active = jax.nn.silu(mixed)
    query = active[..., :DK]
    key = active[..., DK : 2 * DK]
    value = active[..., 2 * DK :]
    query = (
        query * lax.rsqrt(jnp.sum(query * query, axis=-1, keepdims=True) + EPSILON) * DK ** (-0.5)
    )
    key = key * lax.rsqrt(jnp.sum(key * key, axis=-1, keepdims=True) + EPSILON)
    beta = jax.nn.sigmoid(mixer_in[0])
    logdecay = -jnp.exp(decay_log)[:, None] * jax.nn.softplus(mixer_in[1])
    return (query, key, value, beta, logdecay)


def fine(left, right):
    return jnp.matmul(left, right, precision=FINE)


def flip(array):
    return jnp.swapaxes(array, -1, -2)


@jax.custom_vjp
def unit_inverse(lower):
    width = lower.shape[-1]
    row_pos = lax.broadcasted_iota(jnp.int32, (width, width), 0)
    column = lax.broadcasted_iota(jnp.int32, (width, width), 1)

    def pairs(size):
        return (row_pos // size == column // size + 1) & ((row_pos // size) % 2 == 1)

    inverse = jnp.eye(width, dtype=lower.dtype) - jnp.where(pairs(1), lower, 0.0)
    size = 2
    while size < width:
        inverse = inverse - fine(fine(inverse, jnp.where(pairs(size), lower, 0.0)), inverse)
        size *= 2
    return inverse


def unit_inverse_fwd(lower):
    inverse = unit_inverse(lower)
    return inverse, inverse


def unit_inverse_bwd(inverse, grad):
    turned = flip(inverse)
    return (-fine(fine(turned, grad), turned),)


unit_inverse.defvjp(unit_inverse_fwd, unit_inverse_bwd)


def stretch_terms(query, key, value, beta, logdecay):
    width = query.shape[-2]
    row_pos = lax.broadcasted_iota(jnp.int32, (width, width), 0)
    column = lax.broadcasted_iota(jnp.int32, (width, width), 1)
    upto = (row_pos >= column).astype(jnp.float32)
    cumul = jnp.sum(upto * logdecay[..., None, :], axis=-1)
    last = jnp.sum(logdecay, axis=-1)[..., None, None]
    spread = cumul[..., :, None] - cumul[..., None, :]
    decay = jnp.exp(jnp.where(row_pos >= column, spread, NEGATIVE))
    strict = jnp.where(row_pos > column, decay, 0.0)
    lower = beta[..., None] * strict * fine(key, flip(key))
    inverse = unit_inverse(lower)
    growth = jnp.exp(cumul)[..., None]
    sides = jnp.concatenate(
        [(beta[..., None] * growth) * key, beta[..., None] * value], axis=-1
    )
    solved = jnp.matmul(inverse, sides)
    scores = decay * jnp.matmul(query, flip(key))
    mapped = jnp.matmul(scores, solved)
    query_map = growth * query - mapped[..., :DK]
    out_fixed = mapped[..., DK:]
    key_end = jnp.exp(last - cumul[..., None]) * key
    ended = jnp.matmul(flip(key_end), solved)
    transit = jnp.exp(last) * jnp.eye(DK, dtype=query.dtype) - ended[..., :DK]
    feed = ended[..., DK:]
    return (query_map, out_fixed, transit, feed)


def gated(layer_outputs, gate, gain):
    return rms_apply(layer_outputs, gain) * jax.nn.silu(gate)


def swiglu(gate_up):
    return jax.nn.silu(gate_up[:, 0]) * gate_up[:, 1]


def chain(maps, feeds):
    start = jnp.concatenate(
        [
            jnp.broadcast_to(jnp.eye(DK, dtype=jnp.float32), maps[0].shape),
            jnp.zeros_like(feeds[0]),
        ],
        axis=-1,
    )
    pad = ((0, 0), (0, 0), (DK, 0))
    states = [start]
    for index, (part, feed) in enumerate(zip(maps, feeds)):
        if index == 0:
            states.append(jnp.concatenate([part, feed], axis=-1))
        else:
            states.append(fine(part, states[-1]) + jnp.pad(feed, pad))
    return states


def shards(
    block_input,
    norm1_gain,
    w_in,
    w_ba,
    conv_weight,
    decay_log,
    gnorm_gain,
    w_out,
    norm2_gain,
    w_up,
    w_down,
    grad_out,
):
    length = block_input.shape[0]
    heads = w_in.shape[1]
    channels = conv_weight.shape[0]
    blocks = length // STRETCH
    f32 = jnp.float32
    bf16 = jnp.bfloat16

    def split(array):
        return array.reshape((heads, blocks, STRETCH) + array.shape[2:])

    tokens_wide = block_input.astype(f32)
    normed, pull_first = jax.vjp(rms_apply, tokens_wide, norm1_gain)
    normed_b = normed.astype(bf16)
    projected = jnp.einsum(
        "td,dhc->htc", normed_b, w_in, preferred_element_type=f32
    ).astype(bf16)
    mixer_in = jnp.einsum("td,dch->cht", normed_b, w_ba, preferred_element_type=f32)
    edge = shifted(projected[:, length - (CONV - 1) :, :channels], "seq", 1)
    edged = jnp.concatenate([edge, projected[:, :, :channels]], 1).astype(f32)
    feats, pull_feat = jax.vjp(features, edged, mixer_in, conv_weight, decay_log)
    terms, pull_terms = jax.vjp(stretch_terms, *[split(a) for a in feats])
    query_map, out_fixed, transit, feed = terms
    starts = chain(
        [transit[:, i] for i in range(blocks)], [feed[:, i] for i in range(blocks)]
    )
    carried = carried_states(starts[-1], False)
    before = jnp.stack(starts[:-1], axis=1)
    states = jnp.matmul(before[..., :DK], carried[:, None]) + before[..., DK:]
    layer_outputs = (jnp.matmul(query_map, states) + out_fixed).reshape(heads, length, DV)
    gate_wide = projected[:, :, channels:].astype(f32)
    gated_out, pull_gate = jax.vjp(gated, layer_outputs, gate_wide, gnorm_gain)
    gated_b = gated_out.astype(bf16)
    mixer_part = jnp.einsum("htc,chd->td", gated_b, w_out, preferred_element_type=f32)
    mixed = head_sum(mixer_part).astype(f32)
    hidden = tokens_wide + mixed
    hidden_n, pull_second = jax.vjp(rms_apply, hidden, norm2_gain)
    hidden_b = hidden_n.astype(bf16)
    gate_up = jnp.einsum("td,dcf->tcf", hidden_b, w_up, preferred_element_type=f32)
    swish, pull_swish = jax.vjp(swiglu, gate_up)
    swish_b = swish.astype(bf16)
    act_grad = jnp.dot(grad_out, w_down, preferred_element_type=f32)
    (gate_up_grad,) = pull_swish(act_grad)
    gate_up_b = gate_up_grad.astype(bf16)
    second_part = jnp.einsum("tcf,dcf->td", gate_up_b, w_up, preferred_element_type=f32)
    second_total = head_sum(second_part).astype(f32)
    down_grad = lax.dot_general(
        grad_out, swish_b, (((0,), (0,)), ((), ())), preferred_element_type=f32
    )
    up_grad = jnp.einsum("td,tcf->dcf", hidden_b, gate_up_b, preferred_element_type=f32)
    up_share = seq_share(up_grad)
    down_share = seq_share(down_grad)
    hidden_grad, gain_second = pull_second(second_total)
    stream = grad_out.astype(f32) + hidden_grad
    stream_b = stream.astype(bf16)
    gated_grad = jnp.einsum("td,chd->htc", stream_b, w_out, preferred_element_type=f32)
    output_gradient, gate_grad, gain_gated = pull_gate(gated_grad)
    out_weight_grad = jnp.einsum("htc,td->chd", gated_b, stream_b, preferred_element_type=f32)
    out_split = split(output_gradient)
    back_feed = jnp.matmul(flip(query_map), out_split)
    turned = flip(transit)
    backs = chain(
        [turned[:, i] for i in reversed(range(blocks))],
        [back_feed[:, i] for i in reversed(range(blocks))],
    )
    later_grad = carried_states(backs[-1], True)
    after = jnp.stack(backs[:-1][::-1], axis=1)
    later = jnp.matmul(after[..., :DK], later_grad[:, None]) + after[..., DK:]
    term_grad = (
        jnp.matmul(out_split, flip(states)),
        out_split,
        jnp.matmul(later, flip(states)),
        later,
    )
    feat_grad = [
        a.reshape((heads, length) + a.shape[3:]) for a in pull_terms(term_grad)
    ]
    edged_grad, mixer_grad, conv_grad, log_decay_gradient = pull_feat(tuple(feat_grad))
    back_edge = shifted(edged_grad[:, : CONV - 1], "seq", -1)
    channel_grad = edged_grad[:, CONV - 1 :]
    channel_grad = jnp.concatenate(
        [
            channel_grad[:, : length - (CONV - 1)],
            channel_grad[:, length - (CONV - 1) :] + back_edge,
        ],
        1,
    )
    proj_grad = jnp.concatenate([channel_grad, gate_grad], 2).astype(bf16)
    mixer_b = mixer_grad.astype(bf16)
    first_part = jnp.einsum("htc,dhc->td", proj_grad, w_in, preferred_element_type=f32)
    first_part = first_part + jnp.einsum(
        "cht,dch->td", mixer_b, w_ba, preferred_element_type=f32
    )
    first_total = head_sum(first_part).astype(f32)
    ffn_part = lax.dot_general(
        swish_b, w_down, (((1,), (1,)), ((), ())), preferred_element_type=f32
    )
    result = hidden + lax.psum(ffn_part.astype(bf16), "head").astype(f32)
    in_weight_grad = jnp.einsum("td,htc->dhc", normed_b, proj_grad, preferred_element_type=f32)
    in_rows = in_weight_grad.shape[0]
    out_shape = out_weight_grad.shape
    in_share, out_share = seq_shares(
        [
            in_weight_grad.astype(bf16).reshape(in_rows, -1),
            out_weight_grad.astype(bf16).reshape(in_rows, -1),
        ]
    )
    count = lax.axis_size("seq")
    in_share = in_share.reshape((in_rows // count,) + in_weight_grad.shape[1:])
    out_share = out_share.reshape((out_shape[0] // count,) + out_shape[1:])
    gate_weight_grad = jnp.einsum("td,cht->dch", normed_b, mixer_b, preferred_element_type=f32)
    input_part, gain_first = pull_first(first_total)
    input_grad = stream + input_part
    small = [
        gain_first,
        gain_second,
        lax.psum(gain_gated, "head"),
        log_decay_gradient,
        conv_grad.reshape(-1),
        gate_weight_grad.reshape(-1),
    ]
    summed = lax.psum(jnp.concatenate(small), "seq")
    pieces, at = [], 0
    for part in small:
        pieces.append(summed[at : at + part.shape[0]])
        at += part.shape[0]
    gain_one, gain_two, gain_norm, decay_total, conv_total, gate_total = pieces
    count = lax.axis_size("seq")
    place = lax.axis_index("seq")

    def mine(flat, shape):
        share = flat.shape[0] // count
        piece = lax.dynamic_slice(flat, (place * share,), (share,))
        return piece.reshape((shape[0] // count,) + shape[1:])

    return (
        result,
        input_grad,
        gain_one,
        in_share,
        mine(gate_total, gate_weight_grad.shape),
        mine(conv_total, conv_grad.shape),
        decay_total,
        gain_norm,
        out_share,
        gain_two,
        up_share,
        down_share,
    )


def solution(mesh):
    return jax.shard_map(
        shards,
        mesh=mesh,
        in_specs=(
            P("seq", None),
            P(),
            P(None, "head", None),
            P(None, None, "head"),
            P(None, "head", None),
            P("head"),
            P(),
            P(None, "head", None),
            P(),
            P(None, None, "head"),
            P(None, "head"),
            P("seq", None),
        ),
        out_specs=(
            P("seq", None),
            P("seq", None),
            P(),
            P("seq", "head", None),
            P("seq", None, "head"),
            P("seq", "head", None),
            P("head"),
            P(),
            P("seq", "head", None),
            P(),
            P("seq", None, "head"),
            P("seq", "head"),
        ),
        check_vma=False,
    )
```

```python
import functools

import jax
import jax.numpy as jnp
from jax import lax
from jax.experimental import pallas as pl
from jax.experimental.pallas import tpu as pltpu
from jax.sharding import PartitionSpec as P

DK = 128
DV = 256
CONV = 4
STRETCH = 64


EPSILON = 1e-06
NEGATIVE = -1e30
FINE = lax.Precision.HIGH


def shifted(block, axis, distance):
    devices = range(lax.axis_size(axis))
    route = [(i - distance, i) for i in devices if i - distance in devices]
    return lax.ppermute(block, axis, route)


MESH = pl.DeviceIdType.MESH
PIECES = 4


def flipped(index, bit):
    mine = (index // bit) % 2
    return index + bit - 2 * bit * mine, mine


def powers(count):
    return [2**i for i in range(count.bit_length() - 1)]


def greet(axis, partners):
    barrier = pltpu.get_barrier_semaphore()
    for partner in partners:
        pl.semaphore_signal(barrier, inc=1, device_id={axis: partner}, device_id_type=MESH)
    pl.semaphore_wait(barrier, len(partners))


def head_sum_kernel(
    count, x_ref, out_ref, first, held, sums, near_s, near_r, far_s, far_r, back_s, back_r
):
    me = lax.axis_index("head")
    bits = powers(count)
    partner, side = flipped(me, 1)
    peers = [flipped(me, bit)[0] for bit in bits[1:]]
    greet("head", [partner] + peers)

    def send(src, dst, send_sem, recv_sem, device):
        copy = pltpu.make_async_remote_copy(
            src_ref=src,
            dst_ref=dst,
            send_sem=send_sem,
            recv_sem=recv_sem,
            device_id={"head": device},
            device_id_type=MESH,
        )
        copy.start()
        return copy

    def add(left, right):
        return (left.astype(jnp.float32) + right.astype(jnp.float32)).astype(jnp.bfloat16)

    near = [
        send(x_ref.at[1 - side, k], first.at[k], near_s.at[k], near_r.at[k], partner)
        for k in range(PIECES)
    ]
    steps = len(peers)
    copies = []
    for k in range(PIECES):
        near[k].wait()
        sums[0, k] = add(x_ref[side, k], first[k])
        copies.append(
            send(sums.at[0, k], held.at[0, k], far_s.at[0, k], far_r.at[0, k], peers[0])
        )
    for step in range(steps):
        later = []
        for k in range(PIECES):
            copies[k].wait()
            total = add(sums[step, k], held[step, k])
            if step < steps - 1:
                sums[step + 1, k] = total
                later.append(
                    send(
                        sums.at[step + 1, k],
                        held.at[step + 1, k],
                        far_s.at[step + 1, k],
                        far_r.at[step + 1, k],
                        peers[step + 1],
                    )
                )
            else:
                out_ref[side, k] = total
                later.append(
                    send(
                        out_ref.at[side, k],
                        out_ref.at[side, k],
                        back_s.at[k],
                        back_r.at[k],
                        partner,
                    )
                )
        copies = later
    for copy in copies:
        copy.wait()


def head_sum(part):
    count = lax.axis_size("head")
    rows, width = part.shape
    steps = len(powers(count)) - 1
    piece = (rows // (2 * PIECES), width)
    whole = (2, PIECES) + piece
    dma = pltpu.SemaphoreType.DMA
    total = pl.pallas_call(
        functools.partial(head_sum_kernel, count),
        out_shape=jax.ShapeDtypeStruct(whole, jnp.bfloat16),
        in_specs=[pl.BlockSpec(memory_space=pltpu.VMEM)],
        out_specs=pl.BlockSpec(memory_space=pltpu.VMEM),
        scratch_shapes=[
            pltpu.VMEM((PIECES,) + piece, jnp.bfloat16),
            pltpu.VMEM((steps, PIECES) + piece, jnp.bfloat16),
            pltpu.VMEM((steps, PIECES) + piece, jnp.bfloat16),
            dma((PIECES,)),
            dma((PIECES,)),
            dma((steps, PIECES)),
            dma((steps, PIECES)),
            dma((PIECES,)),
            dma((PIECES,)),
        ],
        compiler_params=pltpu.CompilerParams(
            collective_id=0, has_side_effects=True, vmem_limit_bytes=16 << 20
        ),
        name="head_sum",
    )(part.astype(jnp.bfloat16).reshape(whole))
    return total.reshape(rows, width)


def seq_share_kernel(count, arrays, *refs):
    x_refs, out_refs = refs[:arrays], refs[arrays : 2 * arrays]
    scratch = refs[2 * arrays :]
    recv_refs, send_refs = scratch[:arrays], scratch[arrays : 2 * arrays]
    send_sem, recv_sem = scratch[2 * arrays :]
    me = lax.axis_index("seq")
    bits = powers(count)
    partners = {bit: flipped(me, bit)[0] for bit in bits}
    greet("seq", [partners[bit] for bit in bits])

    def block(relative):
        index = me
        for bit in bits:
            if relative & bit:
                index = flipped(index, bit)[0]
        return index

    orders = [bits, bits[1:] + bits[:1]]
    works = []
    for a in range(arrays):
        half = x_refs[a].shape[1] // 2
        for way in range(2):
            works.append((a, way, pl.ds(way * half, half)))

    def kept(order, step):
        used = sum(order[:step])
        return [r for r in range(count) if r & used == 0]

    def partial_sum(work, relative, step):
        a, way, rows = work
        total = x_refs[a][block(relative), rows, :].astype(jnp.float32)
        for earlier in range(step):
            total = total + recv_refs[a][way, earlier, slot(way, earlier, relative)].astype(
                jnp.float32
            )
        return total

    def slot(way, step, relative):
        return kept(orders[way], step + 1).index(relative)

    pending = {}
    for step in range(len(bits) + 1):
        for number, work in enumerate(works):
            a, way, rows = work
            order = orders[way]
            for copy in pending.pop(number, []):
                copy.wait()
            if step == len(bits):
                out_refs[a][rows, :] = partial_sum(work, 0, step)
                continue
            bit = order[step]
            started = []
            for relative in kept(order, step):
                if not relative & bit:
                    continue
                place = slot(way, step, relative - bit)
                if step == 0:
                    source = x_refs[a].at[block(relative), rows, :]
                else:
                    send_refs[a][way, step - 1, place] = partial_sum(
                        work, relative, step
                    ).astype(jnp.bfloat16)
                    source = send_refs[a].at[way, step - 1, place]
                copy = pltpu.make_async_remote_copy(
                    src_ref=source,
                    dst_ref=recv_refs[a].at[way, step, place],
                    send_sem=send_sem.at[number, step, place],
                    recv_sem=recv_sem.at[number, step, place],
                    device_id={"seq": partners[bit]},
                    device_id_type=MESH,
                )
                copy.start()
                started.append(copy)
            pending[number] = started


def seq_shares(grads):
    count = lax.axis_size("seq")
    steps = len(powers(count))
    blocks = [
        g.astype(jnp.bfloat16).reshape(count, g.shape[0] // count, g.shape[1]) for g in grads
    ]
    halves = [(b.shape[1] // 2, b.shape[2]) for b in blocks]
    works = 2 * len(grads)
    vmem = pl.BlockSpec(memory_space=pltpu.VMEM)
    return pl.pallas_call(
        functools.partial(seq_share_kernel, count, len(grads)),
        out_shape=[jax.ShapeDtypeStruct(b.shape[1:], jnp.float32) for b in blocks],
        in_specs=[vmem] * len(grads),
        out_specs=[vmem] * len(grads),
        scratch_shapes=[
            pltpu.VMEM((2, steps, count // 2) + half, jnp.bfloat16) for half in halves
        ]
        + [pltpu.VMEM((2, max(steps - 1, 1), count // 4) + half, jnp.bfloat16) for half in halves]
        + [
            pltpu.SemaphoreType.DMA((works, steps, count // 2)),
            pltpu.SemaphoreType.DMA((works, steps, count // 2)),
        ],
        compiler_params=pltpu.CompilerParams(
            collective_id=1, has_side_effects=True, vmem_limit_bytes=48 << 20
        ),
        name="seq_shares",
    )(*blocks)


def seq_share(grad):
    return lax.psum_scatter(
        grad.astype(jnp.bfloat16), "seq", scatter_dimension=0, tiled=True
    ).astype(jnp.float32)


def carried_states(part, reverse):
    count = lax.axis_size("seq")
    place = lax.axis_index("seq")
    gathered = lax.all_gather(part.astype(jnp.bfloat16), "seq")
    order = range(count - 1, 0, -1) if reverse else range(count - 1)
    state = jnp.zeros(part.shape[:-1] + (DV,), jnp.float32)
    for index, source in enumerate(order):
        feed = gathered[source, ..., DK:].astype(jnp.float32)
        if index:
            moved = (
                jnp.matmul(
                    gathered[source, ..., :DK],
                    state.astype(jnp.bfloat16),
                    preferred_element_type=jnp.float32,
                )
                + feed
            )
        else:
            moved = feed
        ahead = source > place if reverse else source < place
        state = jnp.where(ahead, moved, state)
    return state


def rms_apply(values, gain):
    return values * lax.rsqrt(jnp.mean(values * values, axis=-1, keepdims=True) + EPSILON) * gain


def features(edged, mixer_in, conv_weight, decay_log):
    length = edged.shape[1] - (CONV - 1)
    taps = jnp.transpose(conv_weight, (2, 1, 0))[:, :, None, :]
    mixed = edged[:, 0:length] * taps[0]
    for index in range(1, CONV):
        mixed = mixed + edged[:, index : index + length] * taps[index]
    active = jax.nn.silu(mixed)
    query = active[..., :DK]
    key = active[..., DK : 2 * DK]
    value = active[..., 2 * DK :]
    query = (
        query * lax.rsqrt(jnp.sum(query * query, axis=-1, keepdims=True) + EPSILON) * DK ** (-0.5)
    )
    key = key * lax.rsqrt(jnp.sum(key * key, axis=-1, keepdims=True) + EPSILON)
    beta = jax.nn.sigmoid(mixer_in[0])
    logdecay = -jnp.exp(decay_log)[:, None] * jax.nn.softplus(mixer_in[1])
    return (query, key, value, beta, logdecay)


def fine(left, right):
    return jnp.matmul(left, right, precision=FINE)


def flip(array):
    return jnp.swapaxes(array, -1, -2)


@jax.custom_vjp
def unit_inverse(lower):
    width = lower.shape[-1]
    row_pos = lax.broadcasted_iota(jnp.int32, (width, width), 0)
    column = lax.broadcasted_iota(jnp.int32, (width, width), 1)

    def pairs(size):
        return (row_pos // size == column // size + 1) & ((row_pos // size) % 2 == 1)

    inverse = jnp.eye(width, dtype=lower.dtype) - jnp.where(pairs(1), lower, 0.0)
    size = 2
    while size < width:
        inverse = inverse - fine(fine(inverse, jnp.where(pairs(size), lower, 0.0)), inverse)
        size *= 2
    return inverse


def unit_inverse_fwd(lower):
    inverse = unit_inverse(lower)
    return inverse, inverse


def unit_inverse_bwd(inverse, grad):
    turned = flip(inverse)
    return (-fine(fine(turned, grad), turned),)


unit_inverse.defvjp(unit_inverse_fwd, unit_inverse_bwd)


def stretch_terms(query, key, value, beta, logdecay):
    width = query.shape[-2]
    row_pos = lax.broadcasted_iota(jnp.int32, (width, width), 0)
    column = lax.broadcasted_iota(jnp.int32, (width, width), 1)
    upto = (row_pos >= column).astype(jnp.float32)
    cumul = jnp.sum(upto * logdecay[..., None, :], axis=-1)
    last = jnp.sum(logdecay, axis=-1)[..., None, None]
    spread = cumul[..., :, None] - cumul[..., None, :]
    decay = jnp.exp(jnp.where(row_pos >= column, spread, NEGATIVE))
    strict = jnp.where(row_pos > column, decay, 0.0)
    lower = beta[..., None] * strict * fine(key, flip(key))
    inverse = unit_inverse(lower)
    growth = jnp.exp(cumul)[..., None]
    sides = jnp.concatenate(
        [(beta[..., None] * growth) * key, beta[..., None] * value], axis=-1
    )
    solved = jnp.matmul(inverse, sides)
    scores = decay * jnp.matmul(query, flip(key))
    mapped = jnp.matmul(scores, solved)
    query_map = growth * query - mapped[..., :DK]
    out_fixed = mapped[..., DK:]
    key_end = jnp.exp(last - cumul[..., None]) * key
    ended = jnp.matmul(flip(key_end), solved)
    transit = jnp.exp(last) * jnp.eye(DK, dtype=query.dtype) - ended[..., :DK]
    feed = ended[..., DK:]
    return (query_map, out_fixed, transit, feed)


def gated(layer_outputs, gate, gain):
    return rms_apply(layer_outputs, gain) * jax.nn.silu(gate)


def swiglu(gate_up):
    return jax.nn.silu(gate_up[:, 0]) * gate_up[:, 1]


def chain(maps, feeds):
    start = jnp.concatenate(
        [
            jnp.broadcast_to(jnp.eye(DK, dtype=jnp.float32), maps[0].shape),
            jnp.zeros_like(feeds[0]),
        ],
        axis=-1,
    )
    pad = ((0, 0), (0, 0), (DK, 0))
    states = [start]
    for index, (part, feed) in enumerate(zip(maps, feeds)):
        if index == 0:
            states.append(jnp.concatenate([part, feed], axis=-1))
        else:
            states.append(fine(part, states[-1]) + jnp.pad(feed, pad))
    return states


def shards(
    block_input,
    norm1_gain,
    w_in,
    w_ba,
    conv_weight,
    decay_log,
    gnorm_gain,
    w_out,
    norm2_gain,
    w_up,
    w_down,
    grad_out,
):
    length = block_input.shape[0]
    heads = w_in.shape[1]
    channels = conv_weight.shape[0]
    blocks = length // STRETCH
    f32 = jnp.float32
    bf16 = jnp.bfloat16

    def split(array):
        return array.reshape((heads, blocks, STRETCH) + array.shape[2:])

    tokens_wide = block_input.astype(f32)
    normed, pull_first = jax.vjp(rms_apply, tokens_wide, norm1_gain)
    normed_b = normed.astype(bf16)
    projected = jnp.einsum(
        "td,dhc->htc", normed_b, w_in, preferred_element_type=f32
    ).astype(bf16)
    mixer_in = jnp.einsum("td,dch->cht", normed_b, w_ba, preferred_element_type=f32)
    edge = shifted(projected[:, length - (CONV - 1) :, :channels], "seq", 1)
    edged = jnp.concatenate([edge, projected[:, :, :channels]], 1).astype(f32)
    feats, pull_feat = jax.vjp(features, edged, mixer_in, conv_weight, decay_log)
    terms, pull_terms = jax.vjp(stretch_terms, *[split(a) for a in feats])
    query_map, out_fixed, transit, feed = terms
    starts = chain(
        [transit[:, i] for i in range(blocks)], [feed[:, i] for i in range(blocks)]
    )
    carried = carried_states(starts[-1], False)
    before = jnp.stack(starts[:-1], axis=1)
    states = jnp.matmul(before[..., :DK], carried[:, None]) + before[..., DK:]
    layer_outputs = (jnp.matmul(query_map, states) + out_fixed).reshape(heads, length, DV)
    gate_wide = projected[:, :, channels:].astype(f32)
    gated_out, pull_gate = jax.vjp(gated, layer_outputs, gate_wide, gnorm_gain)
    gated_b = gated_out.astype(bf16)
    mixer_part = jnp.einsum("htc,chd->td", gated_b, w_out, preferred_element_type=f32)
    mixed = head_sum(mixer_part).astype(f32)
    hidden = tokens_wide + mixed
    hidden_n, pull_second = jax.vjp(rms_apply, hidden, norm2_gain)
    hidden_b = hidden_n.astype(bf16)
    gate_up = jnp.einsum("td,dcf->tcf", hidden_b, w_up, preferred_element_type=f32)
    swish, pull_swish = jax.vjp(swiglu, gate_up)
    swish_b = swish.astype(bf16)
    act_grad = jnp.dot(grad_out, w_down, preferred_element_type=f32)
    (gate_up_grad,) = pull_swish(act_grad)
    gate_up_b = gate_up_grad.astype(bf16)
    second_part = jnp.einsum("tcf,dcf->td", gate_up_b, w_up, preferred_element_type=f32)
    second_total = head_sum(second_part).astype(f32)
    down_grad = lax.dot_general(
        grad_out, swish_b, (((0,), (0,)), ((), ())), preferred_element_type=f32
    )
    up_grad = jnp.einsum("td,tcf->dcf", hidden_b, gate_up_b, preferred_element_type=f32)
    hidden_grad, gain_second = pull_second(second_total)
    stream = grad_out.astype(f32) + hidden_grad
    stream_b = stream.astype(bf16)
    gated_grad = jnp.einsum("td,chd->htc", stream_b, w_out, preferred_element_type=f32)
    output_gradient, gate_grad, gain_gated = pull_gate(gated_grad)
    out_weight_grad = jnp.einsum("htc,td->chd", gated_b, stream_b, preferred_element_type=f32)
    out_split = split(output_gradient)
    back_feed = jnp.matmul(flip(query_map), out_split)
    turned = flip(transit)
    backs = chain(
        [turned[:, i] for i in reversed(range(blocks))],
        [back_feed[:, i] for i in reversed(range(blocks))],
    )
    later_grad = carried_states(backs[-1], True)
    later_grad, up_grad, down_grad = lax.optimization_barrier(
        (later_grad, up_grad.astype(bf16), down_grad.astype(bf16))
    )
    up_share = seq_share(up_grad)
    down_share = seq_share(down_grad)
    after = jnp.stack(backs[:-1][::-1], axis=1)
    later = jnp.matmul(after[..., :DK], later_grad[:, None]) + after[..., DK:]
    term_grad = (
        jnp.matmul(out_split, flip(states)),
        out_split,
        jnp.matmul(later, flip(states)),
        later,
    )
    feat_grad = [
        a.reshape((heads, length) + a.shape[3:]) for a in pull_terms(term_grad)
    ]
    edged_grad, mixer_grad, conv_grad, log_decay_gradient = pull_feat(tuple(feat_grad))
    back_edge = shifted(edged_grad[:, : CONV - 1], "seq", -1)
    channel_grad = edged_grad[:, CONV - 1 :]
    channel_grad = jnp.concatenate(
        [
            channel_grad[:, : length - (CONV - 1)],
            channel_grad[:, length - (CONV - 1) :] + back_edge,
        ],
        1,
    )
    proj_grad = jnp.concatenate([channel_grad, gate_grad], 2).astype(bf16)
    mixer_b = mixer_grad.astype(bf16)
    first_part = jnp.einsum("htc,dhc->td", proj_grad, w_in, preferred_element_type=f32)
    first_part = first_part + jnp.einsum(
        "cht,dch->td", mixer_b, w_ba, preferred_element_type=f32
    )
    first_total = head_sum(first_part).astype(f32)
    ffn_part = lax.dot_general(
        swish_b, w_down, (((1,), (1,)), ((), ())), preferred_element_type=f32
    )
    result = hidden + head_sum(ffn_part).astype(f32)
    in_weight_grad = jnp.einsum("td,htc->dhc", normed_b, proj_grad, preferred_element_type=f32)
    in_rows = in_weight_grad.shape[0]
    out_shape = out_weight_grad.shape
    in_share, out_share = seq_shares(
        [
            in_weight_grad.astype(bf16).reshape(in_rows, -1),
            out_weight_grad.astype(bf16).reshape(in_rows, -1),
        ]
    )
    count = lax.axis_size("seq")
    in_share = in_share.reshape((in_rows // count,) + in_weight_grad.shape[1:])
    out_share = out_share.reshape((out_shape[0] // count,) + out_shape[1:])
    gate_weight_grad = jnp.einsum("td,cht->dch", normed_b, mixer_b, preferred_element_type=f32)
    input_part, gain_first = pull_first(first_total)
    input_grad = stream + input_part
    small = [
        gain_first,
        gain_second,
        lax.psum(gain_gated, "head"),
        log_decay_gradient,
        conv_grad.reshape(-1),
        gate_weight_grad.reshape(-1),
    ]
    summed = lax.psum(jnp.concatenate(small), "seq")
    pieces, at = [], 0
    for part in small:
        pieces.append(summed[at : at + part.shape[0]])
        at += part.shape[0]
    gain_one, gain_two, gain_norm, decay_total, conv_total, gate_total = pieces
    count = lax.axis_size("seq")
    place = lax.axis_index("seq")

    def mine(flat, shape):
        share = flat.shape[0] // count
        piece = lax.dynamic_slice(flat, (place * share,), (share,))
        return piece.reshape((shape[0] // count,) + shape[1:])

    return (
        result,
        input_grad,
        gain_one,
        in_share,
        mine(gate_total, gate_weight_grad.shape),
        mine(conv_total, conv_grad.shape),
        decay_total,
        gain_norm,
        out_share,
        gain_two,
        up_share,
        down_share,
    )


def solution(mesh):
    return jax.shard_map(
        shards,
        mesh=mesh,
        in_specs=(
            P("seq", None),
            P(),
            P(None, "head", None),
            P(None, None, "head"),
            P(None, "head", None),
            P("head"),
            P(),
            P(None, "head", None),
            P(),
            P(None, None, "head"),
            P(None, "head"),
            P("seq", None),
        ),
        out_specs=(
            P("seq", None),
            P("seq", None),
            P(),
            P("seq", "head", None),
            P("seq", None, "head"),
            P("seq", "head", None),
            P("head"),
            P(),
            P("seq", "head", None),
            P(),
            P("seq", None, "head"),
            P("seq", "head"),
        ),
        check_vma=False,
    )
```
